32 devices in a mesh: slab: 8 (over z, y), col: 4 (over x, core).
Axes of the slice: x: 2, y: 2, z: 4, core: 2. Of those that a mesh axis runs over, the one named last changes fastest.
Arguments:
- vectors: float32 [64, 8192], P('col', 'slab'), may hold values from -6 to 6
- residual_block: float32 [64, 8192], P('col', 'slab'), may hold values from -0.024 to 0.024
- diag_inverse: float32 [64, 128, 128], P('slab'), may hold values from -0.05 to 1.06
- factor_blocks: float32 [64, 2, 128, 128], P('slab'), may hold values from -0.55 to 0.05
- band_diag: float32 [64, 128, 128], P('slab'), may hold values from -0.45 to 4.45
- band_off: float32 [64, 2, 128, 128], P('slab'), may hold values from -0.65 to 0.15
- band_offsets: int32 [64, 2], P('slab'), may hold values from 1 to 3, as said below
Outputs:
- preconditioned: float32 [64, 8192], P('col', 'slab')
- image: float32 [2, 64, 8192], P(None, 'col', 'slab')
- gram: float32 [2, 2, 64, 2, 64], P(None, None, 'col')
The draws below stay inside these ranges and needn't reach their ends.
Inputs may be any that keep to these rules, and one draw needn't show every extreme that they name: `band_offsets`: each block row's 2 offsets are distinct and increasing.
All inputs are finite; a program needn't handle non-finite values.
Results may differ from the reference program's by a relative error of at most 0.0003.
Values sent between devices are 32-bit elements; how exact they have to be, the bound alone decides.
No kernel may reach another device: no remote copies, remote signals or barrier semaphores. Data moves between devices by JAX's collectives and lax.ppermute only.
A program may use at most 320 MiB of HBM per device.

```python
import jax
import jax.numpy as jnp
from jax import lax

BS = 128
COLS = 64
BW = 3
NNZ = 2
NBLK = 64
NODES = 8192


def noise(key, shape, scale):
    values = jnp.clip(jax.random.normal(key, shape, jnp.float32), -4.0, 4.0) * scale
    return values


def node_rates(key):
    low_rate, high_rate = (0.006, 0.1)
    return jnp.exp(jax.random.uniform(key, (BS,), jnp.float32, jnp.log(low_rate), jnp.log(high_rate)))


def draw_diag_inverse(key, part):
    first, second, third = jax.random.split(key, 3)
    jitter = jax.random.uniform(second, (NBLK, BS), jnp.float32, 0.995, 1.005)
    levels = (1.0 - node_rates(first))[None, :] * jitter
    eye = jnp.eye(BS, dtype=jnp.float32)
    return eye[None] * levels[:, None, :] + noise(third, (NBLK, BS, BS), 0.04 / BS ** 0.5)


def draw_factor_blocks(key, part):
    eye = jnp.eye(BS, dtype=jnp.float32)
    return -0.5 * (eye[None, None] + noise(key, (NBLK, NNZ, BS, BS), 0.04 / BS ** 0.5))


def draw_band_diag(key, part):
    first, second = jax.random.split(key)
    levels = jax.random.uniform(first, (NBLK, BS), jnp.float32, 2.5, 4.0)
    raw = noise(second, (NBLK, BS, BS), 0.3 / BS ** 0.5)
    eye = jnp.eye(BS, dtype=jnp.float32)
    return eye[None] * levels[:, None, :] + (raw + jnp.swapaxes(raw, 1, 2)) * 0.70710678


def draw_band_off(key, part):
    eye = jnp.eye(BS, dtype=jnp.float32)
    return -0.5 * eye[None, None] + noise(key, (NBLK, NNZ, BS, BS), 0.15 / BS ** 0.5)


def draw_band_offsets(key, part):
    first, second = jax.random.split(key)
    lower = jax.random.randint(first, (NBLK,), 1, BW)
    upper = lower + jax.random.randint(second, (NBLK,), 1, BW - lower + 1)
    lower = lower.at[0].set(1)
    upper = upper.at[0].set(BW)
    return jnp.stack([lower, upper], 1).astype(jnp.int32)


def block_scale(own_key, dims, shards, low, top_value):
    factor_of, own = 1.0, jax.random.fold_in(own_key, 6)
    for position, parts in shards:
        heights = jnp.exp(jax.random.uniform(jax.random.fold_in(own, position), (parts,), jnp.float32, low / len(shards), top_value / len(shards)))
        factor_of = factor_of * jnp.repeat(heights, dims[position] // parts).reshape([-1 if axis == position else 1 for axis in range(len(dims))])
    return factor_of


def gaussian(stream_key, shape, deviation, most, pieces=(), kind=jnp.bfloat16):
    values = jax.random.normal(stream_key, shape, jnp.float32) * deviation
    if len(pieces) > 0:
        values = block_scale(stream_key, shape, pieces, -0.22, 0.18) * values
    return jnp.clip(values, min=-most, max=most).astype(kind)


def setup_inputs(seed: int = 0) -> dict:
    seeds = jax.random.split(jax.random.key(seed), 8)
    return {
        "vectors": gaussian(seeds[0], (COLS, NODES), 1.0, 6.0, ((0, 4), (1, 8)), jnp.float32),
        "residual_block": gaussian(seeds[1], (COLS, NODES), 0.004, 0.024, ((0, 4), (1, 8)), jnp.float32),
        "diag_inverse": draw_diag_inverse(jax.random.fold_in(seeds[7], 71), 0),
        "factor_blocks": draw_factor_blocks(jax.random.fold_in(seeds[7], 71), 0),
        "band_diag": draw_band_diag(jax.random.fold_in(seeds[7], 71), 0),
        "band_off": draw_band_off(jax.random.fold_in(seeds[7], 71), 0),
        "band_offsets": draw_band_offsets(jax.random.fold_in(seeds[7], 71), 0),
    }


HI = lax.Precision.HIGHEST


def to_blocks(a):
    return a.reshape(a.shape[0], -1, BS).transpose(1, 0, 2)


def from_blocks(b):
    return b.transpose(1, 0, 2).reshape(b.shape[1], -1)


def apply_band(sblk, adiag, aoff, offsets, head):
    count = sblk.shape[0]
    reach = head.shape[0]
    extended = jnp.concatenate([head, sblk], 0)
    pulled = jnp.zeros((count, offsets.shape[1]) + sblk.shape[1:], jnp.float32)
    for shift_by in range(1, reach + 1):
        picked = (offsets == shift_by).astype(jnp.float32)[:, :, None, None]
        pulled = pulled + picked * extended[reach - shift_by:reach - shift_by + count][:, None]
    result = jnp.einsum('bcy,bxy->bcx', sblk, adiag, precision=HI)
    result = result + jnp.einsum('bkcy,bkxy->bcx', pulled, aoff, precision=HI)
    pushed = jnp.einsum('bcx,bkxy->bkcy', sblk, aoff, precision=HI)
    spread = jnp.zeros((reach + count,) + sblk.shape[1:], jnp.float32)
    for shift_by in range(1, reach + 1):
        picked = (offsets == shift_by).astype(jnp.float32)[:, :, None, None]
        contrib = jnp.sum(picked * pushed, axis=1)
        spread = spread + jnp.pad(contrib, ((reach - shift_by, shift_by), (0, 0), (0, 0)))
    return result + spread[reach:], spread[:reach]


def forward(rblk, dinv, lower, offsets):
    def step(carry, item):
        rhs, dblock, lblock, offs = item
        acc = rhs
        for k in range(NNZ):
            prev = lax.dynamic_index_in_dim(carry, BW - offs[k], 0, keepdims=False)
            acc = acc - jnp.einsum('cy,xy->cx', prev, lblock[k], precision=HI)
        solved = jnp.einsum('cy,xy->cx', acc, dblock, precision=HI)
        return jnp.concatenate([carry[1:], solved[None]], 0), solved

    start = jnp.zeros((BW,) + rblk.shape[1:], jnp.float32)
    _, solved = lax.scan(step, start, (rblk, dinv, lower, offsets))
    return solved


def backward(zblk, dinv, lower, offsets):
    places = jnp.arange(BW, dtype=jnp.int32)

    def step(carry, item):
        rhs, dblock, lblock, offs = item
        solved = jnp.einsum('cy,yx->cx', rhs - carry[0], dblock, precision=HI)
        nxt = jnp.concatenate([carry[1:], jnp.zeros((1,) + rhs.shape, jnp.float32)], 0)
        for k in range(NNZ):
            pushed = jnp.einsum('cx,xy->cy', solved, lblock[k], precision=HI)
            nxt = nxt + jnp.where((places == offs[k] - 1)[:, None, None], pushed[None], 0.0)
        return nxt, solved

    start = jnp.zeros((BW,) + zblk.shape[1:], jnp.float32)
    _, solved = lax.scan(step, start, (zblk, dinv, lower, offsets), reverse=True)
    return solved


def reference(vectors, residual_block, diag_inverse, factor_blocks, band_diag, band_off, band_offsets):
    xblk = to_blocks(vectors)
    zblk = forward(to_blocks(residual_block), diag_inverse, factor_blocks, band_offsets)
    wblk = backward(zblk, diag_inverse, factor_blocks, band_offsets)
    sblk = jnp.concatenate([xblk, wblk], 1)
    head = jnp.zeros((BW,) + sblk.shape[1:], jnp.float32)
    image_blk, _ = apply_band(sblk, band_diag, band_off, band_offsets, head)
    s_all = from_blocks(sblk).reshape(2, COLS, -1)
    image = from_blocks(image_blk).reshape(2, COLS, -1)
    total = s_all.shape[2]
    gram_b = jnp.einsum('pin,qjn->piqj', s_all, s_all, precision=HI) / total
    gram_a = jnp.einsum('pin,qjn->piqj', s_all, image, precision=HI) / total
    return from_blocks(wblk), image, jnp.stack([gram_b, gram_a])
```

```python
import functools

import jax
import jax.numpy as jnp
from jax import lax
from jax.experimental import pallas as pl
from jax.experimental.pallas import tpu as pltpu
from jax.sharding import PartitionSpec as P

BS = 128
BW = 3
TAIL = BW * BS
BF = jnp.bfloat16
F32 = jnp.float32
NN = (((1,), (0,)), ((), ()))
NT = (((1,), (1,)), ((), ()))


def split(a):
    hi = a.astype(BF)
    return hi, (a - hi.astype(F32)).astype(BF)


def mm(a, b, dims):
    return lax.dot_general(a, b, dims, preferred_element_type=F32)


def dot3(a, b, dims):
    (ah, al), (bh, bl) = a, b
    rows = ah.shape[0]
    both = mm(jnp.concatenate([ah, al], 0), bh, dims)
    return both[:rows] + (both[rows:] + mm(ah, bl, dims))


def lanes(parts):
    return jnp.concatenate(parts, 1)


def prep_kernel(offs, d_ref, l_ref, r_ref, mc, nd, mch, ndh, zloc, fh, fl, bh, bl):
    nb = d_ref.shape[0]
    width = r_ref.shape[0]
    rows = TAIL + width
    half = lax.rem(lax.axis_index("col"), 2)
    row = lax.broadcasted_iota(jnp.int32, (rows, BS), 0)
    lane = lax.broadcasted_iota(jnp.int32, (rows, BS), 1)
    for j in range(BW):
        fh[j] = jnp.where(row == lane + j * BS, 1.0, 0.0).astype(BF)
        fl[j] = jnp.zeros((rows, BS), BF)
    for i in range(nb):
        ds = split(d_ref[i])
        lcat = lanes([l_ref[i, 0], l_ref[i, 1]])
        bcat = split(dot3(ds, split(lcat), NN))
        bh[i], bl[i] = bcat
        p1 = BW + i - offs[i, 0]
        p2 = BW + i - offs[i, 1]
        prev = (lanes([fh[p1], fh[p2]]), lanes([fl[p1], fl[p2]]))
        own = dot3(split(r_ref[:, i * BS : (i + 1) * BS]), ds, NT)
        z = -dot3(prev, bcat, NT)
        z = jnp.concatenate([z[:TAIL], z[TAIL:] + own], 0)
        zloc[i] = z[TAIL:]
        zh, zl = split(z)
        fh[BW + i] = zh
        fl[BW + i] = zl
        if i >= nb - BW:
            k = i - (nb - BW)
            mc[:, k * BS : (k + 1) * BS] = z
    hr = TAIL // 2
    start = pl.multiple_of(half * hr, hr)
    mch[:hr] = mc[pl.ds(start, hr), :]
    mch[hr:] = mc[TAIL:, :]
    ah = lanes([fh[BW + i] for i in range(nb)])
    al = lanes([fl[BW + i] for i in range(nb)])
    full = dot3((ah, al), (ah[:TAIL], al[:TAIL]), NT)
    nd[:TAIL] = full[:TAIL]
    nd[TAIL:] = -full[TAIL:]
    ndh[:hr] = nd[pl.ds(start, hr), :]
    ndh[hr:] = nd[TAIL:, :]


def assemble(own, near, other, high, low, vec):
    parity = lax.rem(lax.axis_index("slab"), 2)
    half = lax.rem(lax.axis_index("col"), 2)
    hr = TAIL // 2
    mine, theirs = parity, 1 - parity
    h, l = split(own[:TAIL])
    high[mine], low[mine] = h, l
    vec[mine] = own[TAIL:]
    vec[theirs] = near[hr:]
    for ref, which in ((near, half), (other, 1 - half)):
        h, l = split(ref[:hr])
        at = pl.ds(pl.multiple_of(which * hr, hr), hr)
        high[theirs, at, :] = h
        low[theirs, at, :] = l


def step_rows(x, high, low, slot, dims):
    return dot3(split(x), (high[slot], low[slot]), dims)


def first_kernel(own, near, other, high, low, vec, t_out):
    assemble(own, near, other, high, low, vec)
    t_out[...] = vec[1] + step_rows(vec[0], high, low, 1, NN)


def total(refs):
    out = refs[0][...]
    for ref in refs[1:]:
        out = out + ref[...]
    return out


def forward_kernel(n, *refs):
    got, (high, low, vec, t_out) = refs[:n], refs[n:]
    mid = vec[0] + step_rows(total(got), high, low, 0, NN)
    t_out[...] = vec[1] + step_rows(mid, high, low, 1, NN)


def turn_kernel(n, *refs):
    got = refs[:n]
    own, near, other, mh, ml, c, fh, fl, zloc, e, u_out, z_out, nh, nl, d = refs[n:]
    assemble(own, near, other, nh, nl, d)
    t_in = total(got)
    t_mid = c[0] + step_rows(t_in, mh, ml, 0, NN)
    e_odd = d[1] - step_rows(t_mid, nh, nl, 1, NN)
    e_even = d[0] - step_rows(t_in, nh, nl, 0, NN)
    e[0] = e_even
    e[1] = e_odd
    u_out[...] = step_rows(e_odd, mh, ml, 0, NT) + e_even
    nb = zloc.shape[0]
    odd = lax.rem(lax.axis_index("slab"), 2) == 1
    ts = split(jnp.where(odd, t_mid, t_in))
    for i in range(nb):
        z_out[i] = zloc[i] + dot3(ts, (fh[BW + i, :TAIL], fl[BW + i, :TAIL]), NN)


def backward_kernel(n, *refs):
    got, (high, low, e, u_out) = refs[:n], refs[n:]
    mid = e[1] + step_rows(total(got), high, low, 1, NT)
    u_out[...] = step_rows(mid, high, low, 0, NT) + e[0]


def solve_kernel(n, offs, *refs):
    got, (high, low, e, z, d_ref, bh, bl, off, w, tail, below, q, push) = refs[:n], refs[n:]
    nb = z.shape[0]
    width = z.shape[1]
    odd = lax.rem(lax.axis_index("slab"), 2) == 1
    u_in = total(got)
    u_mid = e[1] + step_rows(u_in, high, low, 1, NT)
    u = jnp.where(odd, u_in, u_mid)
    for i in range(BW):
        q[i] = jnp.zeros((width, BS), F32)
    for i in range(nb):
        q[BW + i] = z[i]
    for j in range(BW):
        q[nb + j] = q[nb + j] - u[:, j * BS : (j + 1) * BS]
    for i in range(nb - 1, -1, -1):
        qs = split(q[BW + i])
        both = dot3(qs, (bh[i], bl[i]), NN)
        for k in range(2):
            at = BW + i - offs[i, k]
            q[at] = q[at] - both[:, k * BS : (k + 1) * BS]
        solved = dot3(qs, split(d_ref[i]), NN)
        w[:, i * BS : (i + 1) * BS] = solved
        if i >= nb - BW:
            j = i - (nb - BW)
            tail[:, j * BS : (j + 1) * BS] = solved
    push_head(offs, w, off, push, below)


def push_head(offs, s, off, push, below):
    width = s.shape[0]
    for j in range(2 * BW):
        push[j] = jnp.zeros((width, BS), F32)
    for i in range(BW):
        ss = split(s[:, i * BS : (i + 1) * BS])
        both = dot3(ss, split(lanes([off[i, 0], off[i, 1]])), NN)
        for k in range(2):
            at = BW + i - offs[i, k]
            push[at] = push[at] + both[:, k * BS : (k + 1) * BS]
    for j in range(BW):
        below[:, j * BS : (j + 1) * BS] = push[j]


def band_local(offs, s, diag, off, ext, acc, img, imt):
    nb = diag.shape[0]
    width = s.shape[0]
    for j in range(BW):
        ext[j] = jnp.zeros((width, BS), F32)
    for j in range(nb + BW):
        acc[j] = jnp.zeros((width, BS), F32)
    for i in range(nb):
        ext[BW + i] = s[:, i * BS : (i + 1) * BS]
    for i in range(nb):
        ss = split(ext[BW + i])
        os = split(lanes([off[i, 0], off[i, 1]]))
        p1 = BW + i - offs[i, 0]
        p2 = BW + i - offs[i, 1]
        pulled = dot3(split(lanes([ext[p1], ext[p2]])), os, NT)
        both = dot3(ss, os, NN)
        acc[BW + i] = acc[BW + i] + pulled
        acc[p1] = acc[p1] + both[:, :BS]
        acc[p2] = acc[p2] + both[:, BS:]
    for i in range(nb):
        ss = split(ext[BW + i])
        ds = split(diag[i])
        cols = slice(i * BS, (i + 1) * BS)
        img[:, cols] = acc[BW + i] + dot3(ss, ds, NT)
        imt[:, cols] = acc[BW + i] + dot3(ss, ds, NN)


def band_x_kernel(offs, s, diag, off, img, imt, tail, below, ext, acc):
    band_local(offs, s, diag, off, ext, acc, img, imt)
    tail[...] = s[:, s.shape[1] - TAIL :]
    for j in range(BW):
        below[:, j * BS : (j + 1) * BS] = acc[j]


def band_w_kernel(offs, s, diag, off, img, imt, ext, acc):
    band_local(offs, s, diag, off, ext, acc, img, imt)


def gram_kernel(count, nodes, offs, *refs):
    xs, ws = refs[:count], refs[count : 2 * count]
    (imgx, imtx, headx, abovex, imgw, imtw, headw, abovew, off, image, gram, left, right, hb) = refs[2 * count :]
    width = xs[0].shape[0]
    size = xs[0].shape[1]
    me = lax.axis_index("col")
    sides = ((imgx, imtx, headx, abovex), (imgw, imtw, headw, abovew))
    for p, (img, imt, head, above) in enumerate(sides):
        rows = slice(p * width, (p + 1) * width)
        for j in range(BW):
            hb[j, rows] = head[:, j * BS : (j + 1) * BS]
            hb[BW + j, rows] = jnp.zeros((width, BS), F32)
        image[p] = img[...]
        image[p, :, size - TAIL :] = img[:, size - TAIL :] + above[...]
        left[(2 + p) * width : (3 + p) * width] = imt[...]
        left[(2 + p) * width : (3 + p) * width, size - TAIL :] = imt[:, size - TAIL :] + above[...]
        own = (xs, ws)[p][0]
        left[rows] = own[...]
        for k in range(count):
            at = jnp.bitwise_xor(me, k)
            right[pl.ds(pl.multiple_of((p * count + at) * width, width), width), :] = (xs, ws)[p][k][...]
    for i in range(BW):
        p1 = BW + i - offs[i, 0]
        p2 = BW + i - offs[i, 1]
        pulled = dot3(split(lanes([hb[p1], hb[p2]])), split(lanes([off[i, 0], off[i, 1]])), NT)
        cols = slice(i * BS, (i + 1) * BS)
        for p in range(2):
            part = pulled[p * width : (p + 1) * width]
            rows = slice((2 + p) * width, (3 + p) * width)
            image[p, :, cols] = image[p, :, cols] + part
            left[rows, cols] = left[rows, cols] + part
    gram[...] = dot3(split(left[...]), split(right[...]), NT) / nodes


def call(kernel, outs, ins, smem=0, scratch=(), flops=10**7):
    specs = [pl.BlockSpec(memory_space=pltpu.SMEM)] * smem
    specs += [pl.BlockSpec(memory_space=pltpu.VMEM)] * (len(ins) - smem)
    shapes = [jax.ShapeDtypeStruct(s, t) for s, t in outs]
    size = sum(a.size * a.dtype.itemsize for a in ins)
    return pl.pallas_call(
        kernel,
        out_shape=shapes,
        in_specs=specs,
        out_specs=[pl.BlockSpec(memory_space=pltpu.VMEM)] * len(shapes),
        scratch_shapes=[pltpu.VMEM(s, t) for s, t in scratch],
        cost_estimate=pl.CostEstimate(flops=flops, bytes_accessed=size, transcendentals=0),
        compiler_params=pltpu.CompilerParams(vmem_limit_bytes=48 * 2**20),
    )(*ins)


def gathered(value, axis):
    count = lax.axis_size(axis)
    parts = {0: value}
    step = count // 2
    while step:
        for k in list(parts):
            parts[k ^ step] = lax.ppermute(parts[k], axis, [(i, i ^ step) for i in range(count)])
        step //= 2
    return [parts[k] for k in range(count)]


def per_device(
    vectors, residual_block, diag_inverse, factor_blocks, band_diag, band_off, band_offsets
):
    width, size = vectors.shape
    nb = size // BS
    slabs = lax.axis_size("slab")
    cols = lax.axis_size("col")
    pairs = slabs // 2
    rows = TAIL + width
    hrows = TAIL // 2 + width
    near = [(i, i ^ 1) for i in range(slabs)]
    cores = [(i, i ^ 1) for i in range(cols)]

    x_all = gathered(vectors, "col")
    mc, nd, mch, ndh, zloc, fh, fl, bh, bl = call(
        prep_kernel,
        [((rows, TAIL), F32)] * 2
        + [((hrows, TAIL), F32)] * 2
        + [((nb, width, BS), F32)]
        + [((nb + BW, rows, BS), BF)] * 2
        + [((nb, BS, 2 * BS), BF)] * 2,
        [band_offsets, diag_inverse, factor_blocks, residual_block],
        smem=1,
        flops=4 * 10**9,
    )
    m_near = lax.ppermute(mch, "slab", near)
    n_near = lax.ppermute(ndh, "slab", near)
    imgx, imtx, tailx, belowx = call(
        band_x_kernel,
        [((width, size), F32)] * 2 + [((width, TAIL), F32)] * 2,
        [band_offsets, vectors, band_diag, band_off],
        smem=1,
        scratch=[((nb + BW, width, BS), F32)] * 2,
        flops=10**9,
    )
    up = [(i, i + 1) for i in range(slabs - 1)]
    down = [(i + 1, i) for i in range(slabs - 1)]
    headx = lax.ppermute(tailx, "slab", up)
    abovex = lax.ppermute(belowx, "slab", down)
    m_other = lax.ppermute(m_near, "col", cores)
    n_other = lax.ppermute(n_near, "col", cores)

    mh, ml, c, t_out = call(
        first_kernel,
        [((2, TAIL, TAIL), BF)] * 2 + [((2, width, TAIL), F32), ((width, TAIL), F32)],
        [mc, m_near, m_other],
        flops=10**8,
    )
    got = []
    for h in range(1, pairs):
        hop = [(2 * h - 2, 2 * h), (2 * h - 1, 2 * h + 1)]
        got.append(lax.ppermute(t_out, "slab", hop))
        if h < pairs - 1:
            (t_out,) = call(
                functools.partial(forward_kernel, len(got)),
                [((width, TAIL), F32)],
                got + [mh, ml, c],
                flops=10**8,
            )
    e, u_out, z = call(
        functools.partial(turn_kernel, len(got)),
        [((2, width, TAIL), F32), ((width, TAIL), F32), ((nb, width, BS), F32)],
        got + [nd, n_near, n_other, mh, ml, c, fh, fl, zloc],
        scratch=[((2, TAIL, TAIL), BF)] * 2 + [((2, width, TAIL), F32)],
        flops=4 * 10**8,
    )
    got = []
    for h in range(pairs - 1, 0, -1):
        hop = [(2 * h, 2 * h - 2), (2 * h + 1, 2 * h - 1)]
        got.append(lax.ppermute(u_out, "slab", hop))
        if h > 1:
            (u_out,) = call(
                functools.partial(backward_kernel, len(got)),
                [((width, TAIL), F32)],
                got + [mh, ml, e],
                flops=10**8,
            )
    w, tailw, beloww = call(
        lambda offs, *refs: solve_kernel(len(got), offs, *refs),
        [((width, size), F32)] + [((width, TAIL), F32)] * 2,
        [band_offsets] + got + [mh, ml, e, z, diag_inverse, bh, bl, band_off],
        smem=1,
        scratch=[((nb + BW, width, BS), F32), ((2 * BW, width, BS), F32)],
        flops=4 * 10**8,
    )
    headw = lax.ppermute(tailw, "slab", up)
    abovew = lax.ppermute(beloww, "slab", down)
    w_all = gathered(w, "col")
    imgw, imtw = call(
        band_w_kernel,
        [((width, size), F32)] * 2,
        [band_offsets, w, band_diag, band_off],
        smem=1,
        scratch=[((nb + BW, width, BS), F32)] * 2,
        flops=10**9,
    )
    image, gram = call(
        functools.partial(gram_kernel, cols, float(size * slabs)),
        [((2, width, size), F32), ((4 * width, 2 * cols * width), F32)],
        [band_offsets]
        + x_all
        + w_all
        + [imgx, imtx, headx, abovex, imgw, imtw, headw, abovew, band_off],
        smem=1,
        scratch=[
            ((4 * width, size), F32),
            ((2 * cols * width, size), F32),
            ((2 * BW, 2 * width, BS), F32),
        ],
        flops=10**9,
    )
    step = 1
    while step < slabs:
        gram = gram + lax.ppermute(gram, "slab", [(i, i ^ step) for i in range(slabs)])
        step *= 2
    return (w, image, gram.reshape(2, 2, width, 2, cols * width))


def solution(mesh):
    in_specs = (
        P("col", "slab"),
        P("col", "slab"),
        P("slab", None, None),
        P("slab", None, None, None),
        P("slab", None, None),
        P("slab", None, None, None),
        P("slab", None),
    )
    out_specs = (P("col", "slab"), P(None, "col", "slab"), P(None, None, "col", None, None))
    return jax.shard_map(
        per_device, mesh=mesh, in_specs=in_specs, out_specs=out_specs, check_vma=False
    )
```

```python
import functools

import jax
import jax.numpy as jnp
from jax import lax
from jax.experimental import pallas as pl
from jax.experimental.pallas import tpu as pltpu
from jax.sharding import PartitionSpec as P


BS = 128
BW = 3
TAIL = BW * BS
BF = jnp.bfloat16
F32 = jnp.float32
NN = (((1,), (0,)), ((), ()))
NT = (((1,), (1,)), ((), ()))


def split(a):
    hi = a.astype(BF)
    return hi, (a - hi.astype(F32)).astype(BF)


def mm(a, b, dims):
    return lax.dot_general(a, b, dims, preferred_element_type=F32)


def dot3(a, b, dims):
    (ah, al), (bh, bl) = a, b
    rows = ah.shape[0]
    both = mm(jnp.concatenate([ah, al], 0), bh, dims)
    return both[:rows] + (both[rows:] + mm(ah, bl, dims))


def lanes(parts):
    return jnp.concatenate(parts, 1)


def prep_kernel(offs_hbm, d_hbm, l_hbm, r_hbm, mc, mch, c_out, zloc, fh, fl, bh, bl, dh, dl, offs, d_ref, l_ref, r_ref, sems, other):
    nb = d_ref.shape[0]
    width = r_ref.shape[0]
    rows = TAIL + width
    copies = [(pltpu.make_async_copy(offs_hbm, offs, other.at[0]), pltpu.make_async_copy(r_hbm, r_ref, other.at[1]))]
    for i in range(nb):
        copies.append(
            (
                pltpu.make_async_copy(d_hbm.at[i], d_ref.at[i], sems.at[0, i]),
                pltpu.make_async_copy(l_hbm.at[i], l_ref.at[i], sems.at[1, i]),
            )
        )
    for pair in copies:
        for copy in pair:
            copy.start()
    half = lax.rem(lax.axis_index("col"), 2)
    row = lax.broadcasted_iota(jnp.int32, (rows, BS), 0)
    lane = lax.broadcasted_iota(jnp.int32, (rows, BS), 1)
    for j in range(BW):
        fh[j] = jnp.where(row == lane + j * BS, 1.0, 0.0).astype(BF)
        fl[j] = jnp.zeros((rows, BS), BF)
    for copy in copies[0]:
        copy.wait()

    def block(i):
        for copy in copies[1 + i]:
            copy.wait()
        ds = split(d_ref[i])
        bcat = split(dot3(ds, split(lanes([l_ref[i, 0], l_ref[i, 1]])), NN))
        bh[i], bl[i] = bcat
        dh[i], dl[i] = ds
        return bcat, dot3(split(r_ref[:, i * BS : (i + 1) * BS]), ds, NT)

    ahead = block(0)
    for i in range(nb):
        bcat, own = ahead
        if i + 1 < nb:
            ahead = block(i + 1)
        p1 = BW + i - offs[0, i]
        p2 = BW + i - offs[1, i]
        prev = (lanes([fh[p1], fh[p2]]), lanes([fl[p1], fl[p2]]))
        z = -dot3(prev, bcat, NT)
        z = jnp.concatenate([z[:TAIL], z[TAIL:] + own], 0)
        zloc[i] = z[TAIL:]
        zh, zl = split(z)
        fh[BW + i] = zh
        fl[BW + i] = zl
        if i >= nb - BW:
            k = i - (nb - BW)
            mc[:, k * BS : (k + 1) * BS] = z
    hr = TAIL // 2
    start = pl.multiple_of(half * hr, hr)
    mch[:hr] = mc[pl.ds(start, hr), :]
    mch[hr:] = mc[TAIL:, :]
    c_out[...] = mc[TAIL:, :]


def energy_kernel(fh, fl, nd, ndh):
    nb = fh.shape[0] - BW
    hr = TAIL // 2
    half = lax.rem(lax.axis_index("col"), 2)
    start = pl.multiple_of(half * hr, hr)
    ah = lanes([fh[BW + i] for i in range(nb)])
    al = lanes([fl[BW + i] for i in range(nb)])
    full = dot3((ah, al), (ah[:TAIL], al[:TAIL]), NT)
    nd[:TAIL] = full[:TAIL]
    nd[TAIL:] = -full[TAIL:]
    ndh[:hr] = nd[pl.ds(start, hr), :]
    ndh[hr:] = nd[TAIL:, :]


def early_kernel(c_got, mc, t_out):
    t_out[...] = mc[TAIL:] + dot3(split(c_got[...]), split(mc[:TAIL]), NN)


def assemble(own, near, other, high, low, vec):
    parity = lax.rem(lax.axis_index("slab"), 2)
    half = lax.rem(lax.axis_index("col"), 2)
    hr = TAIL // 2
    mine, theirs = parity, 1 - parity
    h, l = split(own[:TAIL])
    high[mine], low[mine] = h, l
    vec[mine] = own[TAIL:]
    vec[theirs] = near[hr:]
    for ref, which in ((near, half), (other, 1 - half)):
        h, l = split(ref[:hr])
        at = pl.ds(pl.multiple_of(which * hr, hr), hr)
        high[theirs, at, :] = h
        low[theirs, at, :] = l


def step_rows(x, high, low, slot, dims):
    return dot3(split(x), (high[slot], low[slot]), dims)


def first_kernel(got_a, got_b, own, near, other, high, low, vec, t_out):
    assemble(own, near, other, high, low, vec)
    mid = vec[0] + step_rows(got_a[...] + got_b[...], high, low, 0, NN)
    t_out[...] = vec[1] + step_rows(mid, high, low, 1, NN)


def total(refs):
    out = refs[0][...]
    for ref in refs[1:]:
        out = out + ref[...]
    return out


def forward_kernel(n, *refs):
    got, (high, low, vec, t_out) = refs[:n], refs[n:]
    mid = vec[0] + step_rows(total(got), high, low, 0, NN)
    t_out[...] = vec[1] + step_rows(mid, high, low, 1, NN)


def turn_kernel(n, *refs):
    got, (mh, ml, c, nh, nl, d, e, u_out) = refs[:n], refs[n:]
    t_in = total(got)
    t_mid = c[0] + step_rows(t_in, mh, ml, 0, NN)
    e_odd = d[1] - step_rows(t_mid, nh, nl, 1, NN)
    e_even = d[0] - step_rows(t_in, nh, nl, 0, NN)
    e[0] = e_even
    e[1] = e_odd
    u_out[...] = step_rows(e_odd, mh, ml, 0, NT) + e_even


def inner_kernel(n, *refs):
    got, (mh, ml, c, fh, fl, zloc, z_out) = refs[:n], refs[n:]
    t_in = total(got)
    t_mid = c[0] + step_rows(t_in, mh, ml, 0, NN)
    odd = lax.rem(lax.axis_index("slab"), 2) == 1
    ts = split(jnp.where(odd, t_mid, t_in))
    for i in range(zloc.shape[0]):
        z_out[i] = zloc[i] + dot3(ts, (fh[BW + i, :TAIL], fl[BW + i, :TAIL]), NN)


def backward_kernel(n, *refs):
    got, (high, low, e, u_out) = refs[:n], refs[n:]
    mid = e[1] + step_rows(total(got), high, low, 1, NT)
    u_out[...] = step_rows(mid, high, low, 0, NT) + e[0]


def upward_kernel(offs, z, dh, dl, bh, bl, kh, kl, v, q):
    nb, width = z.shape[:2]
    row = lax.broadcasted_iota(jnp.int32, (TAIL, BS), 0)
    lane = lax.broadcasted_iota(jnp.int32, (TAIL, BS), 1)
    for i in range(nb + BW):
        q[i, :TAIL] = jnp.zeros((TAIL, BS), F32)
        if i >= nb:
            q[i, :TAIL] = jnp.where(row == lane + (i - nb) * BS, -1.0, 0.0)
        q[i, TAIL:] = z[i - BW] if i >= BW else jnp.zeros((width, BS), F32)
    for i in range(nb - 1, -1, -1):
        qs = split(q[BW + i])
        both = dot3(qs, (bh[i], bl[i]), NN)
        for k in range(2):
            at = BW + i - offs[k, i]
            q[at] = q[at] - both[:, k * BS : (k + 1) * BS]
        solved = dot3(qs, (dh[i], dl[i]), NN)
        cols = slice(i * BS, (i + 1) * BS)
        v[:, cols] = solved[TAIL:]
        kh[:, cols], kl[:, cols] = split(solved[:TAIL])


def solve_kernel(n, offs, *refs):
    got, (high, low, e, v, kh, kl, oh, ol, x, belowx, w, inner, tail, below, push) = refs[:n], refs[n:]
    width, size = v.shape
    odd = lax.rem(lax.axis_index("slab"), 2) == 1
    u_in = total(got)
    u_mid = e[1] + step_rows(u_in, high, low, 1, NT)
    u = jnp.where(odd, u_in, u_mid)
    solved = v[...] + dot3(split(u), (kh[...], kl[...]), NN)
    w[...] = solved
    inner[...] = solved
    tail[:width] = x[:, size - TAIL :]
    tail[width:] = solved[:, size - TAIL :]
    front = [solved[:, i * BS : (i + 1) * BS] for i in range(BW)]
    push_head(offs, front, oh, ol, push)
    below[:width] = belowx[...]
    for j in range(BW):
        below[width:, j * BS : (j + 1) * BS] = push[j]


def band_local(offs, s, ah, al, oh, ol, ext, acc, img, imt):
    nb = ah.shape[0]
    width = s.shape[0]
    for j in range(BW):
        ext[j] = jnp.zeros((width, BS), F32)
    for j in range(nb + BW):
        acc[j] = jnp.zeros((width, BS), F32)
    for i in range(nb):
        ext[BW + i] = s[:, i * BS : (i + 1) * BS]
    for i in range(nb):
        ss = split(ext[BW + i])
        os = (oh[i], ol[i])
        p1 = BW + i - offs[0, i]
        p2 = BW + i - offs[1, i]
        pulled = dot3(split(lanes([ext[p1], ext[p2]])), os, NT)
        both = dot3(ss, os, NN)
        acc[BW + i] = acc[BW + i] + pulled
        acc[p1] = acc[p1] + both[:, :BS]
        acc[p2] = acc[p2] + both[:, BS:]
    for i in range(nb):
        ss = split(ext[BW + i])
        ds = (ah[i], al[i])
        cols = slice(i * BS, (i + 1) * BS)
        img[:, cols] = acc[BW + i] + dot3(ss, ds, NT)
        imt[:, cols] = acc[BW + i] + dot3(ss, ds, NN)


def band_x_kernel(offs, s, a_hbm, o_hbm, img, imt, below, ah, al, oh, ol, ext, acc, a_ref, o_ref, sems):
    copies = (
        pltpu.make_async_copy(o_hbm, o_ref, sems.at[0]),
        pltpu.make_async_copy(a_hbm, a_ref, sems.at[1]),
    )
    for copy in copies:
        copy.start()
    for copy in copies:
        copy.wait()
    for i in range(ah.shape[0]):
        oh[i], ol[i] = split(lanes([o_ref[i, 0], o_ref[i, 1]]))
        ah[i], al[i] = split(a_ref[i])
    band_local(offs, s, ah, al, oh, ol, ext, acc, img, imt)
    for j in range(BW):
        below[:, j * BS : (j + 1) * BS] = acc[j]


def band_w_kernel(offs, s, ah, al, oh, ol, img, imt, ext, acc):
    band_local(offs, s, ah, al, oh, ol, ext, acc, img, imt)


def push_head(offs, s, oh, ol, push):
    for j in range(2 * BW):
        push[j] = jnp.zeros(push.shape[1:], F32)
    for i in range(BW):
        both = dot3(split(s[i]), (oh[i], ol[i]), NN)
        for k in range(2):
            at = BW + i - offs[k, i]
            push[at] = push[at] + both[:, k * BS : (k + 1) * BS]


def gram_kernel(count, nodes, offs, *refs):
    xs, ws = refs[:count], refs[count : 2 * count]
    (imgx, imtx, imgw, imtw, head, above, oh, ol, image, gram, left, right, hb) = refs[2 * count :]
    width = xs[0].shape[0]
    size = xs[0].shape[1]
    me = lax.axis_index("col")
    for j in range(BW):
        hb[j] = head[:, j * BS : (j + 1) * BS]
        hb[BW + j] = jnp.zeros((2 * width, BS), F32)
    for p, (img, imt) in enumerate(((imgx, imtx), (imgw, imtw))):
        rows = slice(p * width, (p + 1) * width)
        image[p] = img[...]
        image[p, :, size - TAIL :] = img[:, size - TAIL :] + above[rows]
        left[(2 + p) * width : (3 + p) * width] = imt[...]
        left[(2 + p) * width : (3 + p) * width, size - TAIL :] = imt[:, size - TAIL :] + above[rows]
        own = (xs, ws)[p][0]
        left[rows] = own[...]
        for k in range(count):
            at = jnp.bitwise_xor(me, k)
            right[pl.ds(pl.multiple_of((p * count + at) * width, width), width), :] = (xs, ws)[p][k][...]
    for i in range(BW):
        p1 = BW + i - offs[0, i]
        p2 = BW + i - offs[1, i]
        pulled = dot3(split(lanes([hb[p1], hb[p2]])), (oh[i], ol[i]), NT)
        cols = slice(i * BS, (i + 1) * BS)
        for p in range(2):
            part = pulled[p * width : (p + 1) * width]
            rows = slice((2 + p) * width, (3 + p) * width)
            image[p, :, cols] = image[p, :, cols] + part
            left[rows, cols] = left[rows, cols] + part
    gram[...] = dot3(split(left[...]), split(right[...]), NT) / nodes


def sum_kernel(*refs):
    parts, out = refs[:-1], refs[-1]
    whole = total(parts)
    width, half = out.shape[2], out.shape[4]
    for g in range(2):
        for p in range(2):
            at = (2 * g + p) * width
            for q in range(2):
                out[g, p, :, q, :] = whole[at : at + width, q * half : (q + 1) * half]


def call(kernel, outs, ins, smem=0, anys=0, last=0, scratch=(), flops=10**7):
    specs = [pl.BlockSpec(memory_space=pltpu.HBM)] * anys
    specs += [pl.BlockSpec(memory_space=pltpu.SMEM)] * smem
    specs += [pl.BlockSpec(memory_space=pltpu.VMEM)] * (len(ins) - smem - anys - last)
    specs += [pl.BlockSpec(memory_space=pltpu.HBM)] * last
    shapes = [jax.ShapeDtypeStruct(s, t) for s, t in outs]
    size = sum(a.size * a.dtype.itemsize for a in ins)
    return pl.pallas_call(
        kernel,
        out_shape=shapes,
        in_specs=specs,
        out_specs=[pl.BlockSpec(memory_space=pltpu.VMEM)] * len(shapes),
        scratch_shapes=scratch,
        cost_estimate=pl.CostEstimate(flops=flops, bytes_accessed=size, transcendentals=0),
        compiler_params=pltpu.CompilerParams(vmem_limit_bytes=32 * 2**20),
    )(*ins)


def gathered(value, axis):
    count = lax.axis_size(axis)
    parts = {0: value}
    step = count // 2
    while step:
        for k in list(parts):
            links = [(i, i ^ step) for i in range(count)]
            parts[k ^ step] = lax.ppermute(parts[k], axis, links)
        step //= 2
    return [parts[k] for k in range(count)]


def local_program(
    vectors, residual_block, diag_inverse, factor_blocks, band_diag, band_off, band_offsets
):
    width, size = vectors.shape
    nb = size // BS
    offsets = band_offsets.T
    slabs = lax.axis_size("slab")
    cols = lax.axis_size("col")
    pairs = slabs // 2
    rows = TAIL + width
    hrows = TAIL // 2 + width
    near = [(i, i ^ 1) for i in range(slabs)]
    cores = [(i, i ^ 1) for i in range(cols)]
    vec = ((width, TAIL), F32)
    flat = ((width, size), F32)
    matrix = [((2, TAIL, TAIL), BF)] * 2 + [((2, width, TAIL), F32)]

    mc, mch, c_own, zloc, fh, fl, bh, bl, dh, dl = call(
        prep_kernel,
        [((rows, TAIL), F32), ((hrows, TAIL), F32), vec, ((nb, width, BS), F32)]
        + [((nb + BW, rows, BS), BF)] * 2
        + [((nb, BS, 2 * BS), BF)] * 2
        + [((nb, BS, BS), BF)] * 2,
        [
            pltpu.with_memory_space_constraint(a, pltpu.HBM)
            for a in (offsets, diag_inverse, factor_blocks, residual_block)
        ],
        anys=4,
        scratch=[
            pltpu.SMEM(offsets.shape, jnp.int32),
            pltpu.VMEM(diag_inverse.shape, F32),
            pltpu.VMEM(factor_blocks.shape, F32),
            pltpu.VMEM(residual_block.shape, F32),
            pltpu.SemaphoreType.DMA((2, nb)),
            pltpu.SemaphoreType.DMA((2,)),
        ],
        flops=4 * 10**9,
    )
    c_got = lax.ppermute(c_own, "slab", [(0, 1)])
    m_near = lax.ppermute(mch, "slab", near)
    band_scratch = [pltpu.VMEM((nb + BW, width, BS), F32)] * 2
    imgx, imtx, belowx, ah, al, oh, ol = call(
        band_x_kernel,
        [flat, flat, vec] + [((nb, BS, BS), BF)] * 2 + [((nb, BS, 2 * BS), BF)] * 2,
        [offsets, vectors]
        + [pltpu.with_memory_space_constraint(a, pltpu.HBM) for a in (band_diag, band_off)],
        smem=1,
        last=2,
        scratch=band_scratch
        + [
            pltpu.VMEM(band_diag.shape, F32),
            pltpu.VMEM(band_off.shape, F32),
            pltpu.SemaphoreType.DMA((2,)),
        ],
        flops=10**9,
    )
    (t_out,) = call(early_kernel, [vec], [c_got, mc], flops=10**8)
    got_a = lax.ppermute(t_out, "slab", [(1, 3)])
    got_b = lax.ppermute(t_out, "slab", [(1, 2)])
    nd, ndh = call(
        energy_kernel, [((rows, TAIL), F32), ((hrows, TAIL), F32)], [fh, fl], flops=10**9
    )
    n_near = lax.ppermute(ndh, "slab", near)
    x_all = gathered(vectors, "col")
    up = [(i, i + 1) for i in range(slabs - 1)]
    down = [(i + 1, i) for i in range(slabs - 1)]
    m_other = lax.ppermute(m_near, "col", cores)
    n_other = lax.ppermute(n_near, "col", cores)

    mh, ml, c, t_out = call(
        first_kernel, matrix + [vec], [got_a, got_b, mc, m_near, m_other], flops=10**8
    )
    nh, nl, d = call(assemble, matrix, [nd, n_near, n_other], flops=10**8)
    got = [got_a, got_b]
    for h in range(2, pairs):
        hop = [(2 * h - 2, 2 * h), (2 * h - 1, 2 * h + 1)]
        got.append(lax.ppermute(t_out, "slab", hop))
        if h < pairs - 1:
            kernel = functools.partial(forward_kernel, len(got))
            (t_out,) = call(kernel, [vec], got + [mh, ml, c], flops=10**8)
    e, u_out = call(
        functools.partial(turn_kernel, len(got)),
        [((2, width, TAIL), F32), vec],
        got + [mh, ml, c, nh, nl, d],
        flops=10**8,
    )
    (z,) = call(
        functools.partial(inner_kernel, len(got)),
        [((nb, width, BS), F32)],
        got + [mh, ml, c, fh, fl, zloc],
        flops=2 * 10**8,
    )
    got = []
    for h in range(pairs - 1, 0, -1):
        hop = [(2 * h, 2 * h - 2), (2 * h + 1, 2 * h - 1)]
        got.append(lax.ppermute(u_out, "slab", hop))
        if h > 1:
            kernel = functools.partial(backward_kernel, len(got))
            (u_out,) = call(kernel, [vec], got + [mh, ml, e], flops=10**8)
    n_got = len(got)

    def last_kernel(offs, *refs):
        solve_kernel(n_got, offs, *refs)

    kh, kl, v = call(
        upward_kernel,
        [((TAIL, size), BF)] * 2 + [flat],
        [offsets, z, dh, dl, bh, bl],
        smem=1,
        scratch=[pltpu.VMEM((nb + BW, rows, BS), F32)],
        flops=4 * 10**9,
    )
    halo = ((2 * width, TAIL), F32)
    w, inner, tail, below = call(
        last_kernel,
        [flat, flat, halo, halo],
        [offsets] + got + [mh, ml, e, v, kh, kl, oh, ol, vectors, belowx],
        smem=1,
        scratch=[pltpu.VMEM((2 * BW, width, BS), F32)],
        flops=4 * 10**8,
    )
    w_all = gathered(inner, "col")
    head = lax.ppermute(tail, "slab", up)
    above = lax.ppermute(below, "slab", down)
    imgw, imtw = call(
        band_w_kernel,
        [flat, flat],
        [offsets, inner, ah, al, oh, ol],
        smem=1,
        scratch=band_scratch,
        flops=10**9,
    )
    image, gram = call(
        functools.partial(gram_kernel, cols, float(size * slabs)),
        [((2, width, size), F32), ((4 * width, 2 * cols * width), F32)],
        [offsets]
        + x_all
        + w_all
        + [imgx, imtx, imgw, imtw, head, above, oh, ol],
        smem=1,
        scratch=[
            pltpu.VMEM((4 * width, size), F32),
            pltpu.VMEM((2 * cols * width, size), F32),
            pltpu.VMEM((2 * BW, 2 * width, BS), F32),
        ],
        flops=10**9,
    )
    step = 1
    while step < slabs // 4:
        links = [(i, i ^ step) for i in range(slabs)]
        gram = gram + lax.ppermute(gram, "slab", links)
        step *= 2
    parts = [gram]
    for far in (step, 2 * step, 3 * step):
        parts.append(lax.ppermute(gram, "slab", [(i, i ^ far) for i in range(slabs)]))
    (gram,) = call(sum_kernel, [((2, 2, width, 2, cols * width), F32)], parts, flops=10**6)
    return (w, image, gram)


def solution(mesh):
    in_specs = (
        P("col", "slab"),
        P("col", "slab"),
        P("slab", None, None),
        P("slab", None, None, None),
        P("slab", None, None),
        P("slab", None, None, None),
        P("slab", None),
    )
    out_specs = (P("col", "slab"), P(None, "col", "slab"), P(None, None, "col", None, None))
    return jax.shard_map(
        local_program, mesh=mesh, in_specs=in_specs, out_specs=out_specs, check_vma=False
    )
```

```python
import functools

import jax
import jax.numpy as jnp
from jax import lax
from jax.experimental import pallas as pl
from jax.experimental.pallas import tpu as pltpu
from jax.sharding import PartitionSpec as P


BS = 128
BW = 3
TAIL = BW * BS
BF = jnp.bfloat16
F32 = jnp.float32
NN = (((1,), (0,)), ((), ()))
NT = (((1,), (1,)), ((), ()))


def split(a):
    hi = a.astype(BF)
    return hi, (a - hi.astype(F32)).astype(BF)


def mm(a, b, dims):
    return lax.dot_general(a, b, dims, preferred_element_type=F32)


def dot3(a, b, dims):
    (ah, al), (bh, bl) = a, b
    rows, depth = ah.shape
    if depth <= BS:
        axis = dims[0][1][0]
        twice = mm(jnp.concatenate([ah, al], 1), jnp.concatenate([bh, bh], axis), dims)
        return twice + mm(ah, bl, dims)
    both = mm(jnp.concatenate([ah, al], 0), bh, dims)
    return both[:rows] + (both[rows:] + mm(ah, bl, dims))


def lanes(parts):
    return jnp.concatenate(parts, 1)


def prep_kernel(offs_hbm, d_hbm, l_hbm, r_hbm, mc, mch, c_out, zloc, fh, fl, bh, bl, dh, dl, offs, d_ref, l_ref, r_ref, sems, other):
    nb = d_ref.shape[0]
    width = r_ref.shape[0]
    rows = TAIL + width
    copies = [(pltpu.make_async_copy(offs_hbm, offs, other.at[0]), pltpu.make_async_copy(r_hbm, r_ref, other.at[1]))]
    for i in range(nb):
        copies.append(
            (
                pltpu.make_async_copy(d_hbm.at[i], d_ref.at[i], sems.at[0, i]),
                pltpu.make_async_copy(l_hbm.at[i], l_ref.at[i], sems.at[1, i]),
            )
        )
    for pair in copies:
        for copy in pair:
            copy.start()
    half = lax.rem(lax.axis_index("col"), 2)
    row = lax.broadcasted_iota(jnp.int32, (rows, BS), 0)
    lane = lax.broadcasted_iota(jnp.int32, (rows, BS), 1)
    for j in range(BW):
        fh[j] = jnp.where(row == lane + j * BS, 1.0, 0.0).astype(BF)
        fl[j] = jnp.zeros((rows, BS), BF)
    for copy in copies[0]:
        copy.wait()

    def block(i):
        for copy in copies[1 + i]:
            copy.wait()
        ds = split(d_ref[i])
        bcat = split(dot3(ds, split(lanes([l_ref[i, 0], l_ref[i, 1]])), NN))
        bh[i], bl[i] = bcat
        dh[i], dl[i] = ds
        return bcat, dot3(split(r_ref[:, i * BS : (i + 1) * BS]), ds, NT)

    ahead = block(0)
    for i in range(nb):
        bcat, own = ahead
        if i + 1 < nb:
            ahead = block(i + 1)
        p1 = BW + i - offs[0, i]
        p2 = BW + i - offs[1, i]
        prev = (lanes([fh[p1], fh[p2]]), lanes([fl[p1], fl[p2]]))
        z = -dot3(prev, bcat, NT)
        z = jnp.concatenate([z[:TAIL], z[TAIL:] + own], 0)
        zloc[i] = z[TAIL:]
        zh, zl = split(z)
        fh[BW + i] = zh
        fl[BW + i] = zl
        if i >= nb - BW:
            k = i - (nb - BW)
            mc[:, k * BS : (k + 1) * BS] = z
    hr = TAIL // 2
    start = pl.multiple_of(half * hr, hr)
    mch[:hr] = mc[pl.ds(start, hr), :]
    mch[hr:] = mc[TAIL:, :]
    c_out[...] = mc[TAIL:, :]


def energy_kernel(fh, fl, nd, ndh):
    nb = fh.shape[0] - BW
    hr = TAIL // 2
    half = lax.rem(lax.axis_index("col"), 2)
    start = pl.multiple_of(half * hr, hr)
    ah = lanes([fh[BW + i] for i in range(nb)])
    al = lanes([fl[BW + i] for i in range(nb)])
    full = dot3((ah, al), (ah[:TAIL], al[:TAIL]), NT)
    nd[:TAIL] = full[:TAIL]
    nd[TAIL:] = -full[TAIL:]
    ndh[:hr] = nd[pl.ds(start, hr), :]
    ndh[hr:] = nd[TAIL:, :]


def early_kernel(c_got, mc, t_out):
    t_out[...] = mc[TAIL:] + dot3(split(c_got[...]), split(mc[:TAIL]), NN)


def assemble(own, near, other, high, low, vec):
    parity = lax.rem(lax.axis_index("slab"), 2)
    half = lax.rem(lax.axis_index("col"), 2)
    hr = TAIL // 2
    mine, theirs = parity, 1 - parity
    h, l = split(own[:TAIL])
    high[mine], low[mine] = h, l
    vec[mine] = own[TAIL:]
    vec[theirs] = near[hr:]
    for ref, which in ((near, half), (other, 1 - half)):
        h, l = split(ref[:hr])
        at = pl.ds(pl.multiple_of(which * hr, hr), hr)
        high[theirs, at, :] = h
        low[theirs, at, :] = l


def step_rows(x, high, low, slot, dims):
    return dot3(split(x), (high[slot], low[slot]), dims)


def first_kernel(got_a, got_b, own, near, other, high, low, vec, t_out):
    assemble(own, near, other, high, low, vec)
    mid = vec[0] + step_rows(got_a[...] + got_b[...], high, low, 0, NN)
    t_out[...] = vec[1] + step_rows(mid, high, low, 1, NN)


def total(refs):
    out = refs[0][...]
    for ref in refs[1:]:
        out = out + ref[...]
    return out


def forward_kernel(n, *refs):
    got, (high, low, vec, t_out) = refs[:n], refs[n:]
    mid = vec[0] + step_rows(total(got), high, low, 0, NN)
    t_out[...] = vec[1] + step_rows(mid, high, low, 1, NN)


def compose_kernel(high, low, half_out):
    hr = TAIL // 2
    start = pl.multiple_of(lax.rem(lax.axis_index("col"), 2) * hr, hr)
    mine = (high[0, pl.ds(start, hr), :], low[0, pl.ds(start, hr), :])
    half_out[...] = dot3(mine, (high[1], low[1]), NN)


def join_kernel(near, other, high, low):
    half = lax.rem(lax.axis_index("col"), 2)
    hr = TAIL // 2
    for ref, which in ((near, half), (other, 1 - half)):
        h, l = split(ref[...])
        at = pl.ds(pl.multiple_of(which * hr, hr), hr)
        high[at, :] = h
        low[at, :] = l


def turn_kernel(n, *refs):
    got, (mh, ml, c, nh, nl, d, e, u_out) = refs[:n], refs[n:]
    t_in = total(got)
    t_mid = c[0] + step_rows(t_in, mh, ml, 0, NN)
    e_odd = d[1] - step_rows(t_mid, nh, nl, 1, NN)
    e_even = d[0] - step_rows(t_in, nh, nl, 0, NN)
    e[0] = e_even
    e[1] = e_odd
    u_out[...] = step_rows(e_odd, mh, ml, 0, NT) + e_even


def inner_kernel(n, *refs):
    got, (mh, ml, c, fh, fl, zloc, z_out) = refs[:n], refs[n:]
    t_in = total(got)
    t_mid = c[0] + step_rows(t_in, mh, ml, 0, NN)
    odd = lax.rem(lax.axis_index("slab"), 2) == 1
    ts = split(jnp.where(odd, t_mid, t_in))
    for i in range(zloc.shape[0]):
        z_out[i] = zloc[i] + dot3(ts, (fh[BW + i, :TAIL], fl[BW + i, :TAIL]), NN)


def backward_kernel(n, *refs):
    got, (high, low, e, u_out) = refs[:n], refs[n:]
    mid = e[1] + step_rows(total(got), high, low, 1, NT)
    u_out[...] = step_rows(mid, high, low, 0, NT) + e[0]


def upward_steps(offs, dh, dl, bh, bl, q, kh, kl, v, blocks):
    first = blocks[0]
    for i in reversed(blocks):
        qs = split(q[BW + i])
        both = dot3(qs, (bh[i], bl[i]), NN)
        for k in range(2):
            at = BW + i - offs[k, i]
            q[at] = q[at] - both[:, k * BS : (k + 1) * BS]
        solved = dot3(qs, (dh[i], dl[i]), NN)
        cols = slice((i - first) * BS, (i - first + 1) * BS)
        v[:, cols] = solved[TAIL:]
        kh[:, cols], kl[:, cols] = split(solved[:TAIL])


def upward_kernel(offs, z, dh, dl, bh, bl, q, kh, kl, v):
    nb, width = z.shape[:2]
    row = lax.broadcasted_iota(jnp.int32, (TAIL, BS), 0)
    lane = lax.broadcasted_iota(jnp.int32, (TAIL, BS), 1)
    for i in range(nb + BW):
        q[i, :TAIL] = jnp.zeros((TAIL, BS), F32)
        if i >= nb:
            q[i, :TAIL] = jnp.where(row == lane + (i - nb) * BS, -1.0, 0.0)
        q[i, TAIL:] = z[i - BW] if i >= BW else jnp.zeros((width, BS), F32)
    upward_steps(offs, dh, dl, bh, bl, q, kh, kl, v, range(nb // 2, nb))


def upward_rest_kernel(offs, q_in, dh, dl, bh, bl, kh, kl, v, q):
    nb = dh.shape[0]
    for i in range(nb // 2 + BW):
        q[i] = q_in[i]
    upward_steps(offs, dh, dl, bh, bl, q, kh, kl, v, range(nb // 2))


def solve_kernel(n, offs, *refs):
    got, rest = refs[:n], refs[n:]
    (skip, ph, plow, high, low, e, va, kha, kla, vb, khb, klb, oh, ol, x, belowx) = rest[:16]
    (w, inner, tail, below, push) = rest[16:]
    width, size = x.shape
    odd = lax.rem(lax.axis_index("slab"), 2) == 1
    u_in = total(got) + dot3(split(skip[...]), (ph[...], plow[...]), NT)
    u_mid = e[1] + step_rows(u_in, high, low, 1, NT)
    u = jnp.where(odd, u_in, u_mid)
    us = split(u)
    solved = lanes(
        [
            vb[...] + dot3(us, (khb[...], klb[...]), NN),
            va[...] + dot3(us, (kha[...], kla[...]), NN),
        ]
    )
    w[...] = solved
    inner[...] = solved
    tail[:width] = x[:, size - TAIL :]
    tail[width:] = solved[:, size - TAIL :]
    front = [solved[:, i * BS : (i + 1) * BS] for i in range(BW)]
    push_head(offs, front, oh, ol, push)
    below[:width] = belowx[...]
    for j in range(BW):
        below[width:, j * BS : (j + 1) * BS] = push[j]


def band_local(offs, s, ah, al, oh, ol, ext, acc, img, imt):
    nb = ah.shape[0]
    width = s.shape[0]
    for j in range(BW):
        ext[j] = jnp.zeros((width, BS), F32)
    for j in range(nb + BW):
        acc[j] = jnp.zeros((width, BS), F32)
    for i in range(nb):
        ext[BW + i] = s[:, i * BS : (i + 1) * BS]
    for i in range(nb):
        ss = split(ext[BW + i])
        os = (oh[i], ol[i])
        p1 = BW + i - offs[0, i]
        p2 = BW + i - offs[1, i]
        pulled = dot3(split(lanes([ext[p1], ext[p2]])), os, NT)
        both = dot3(ss, os, NN)
        acc[BW + i] = acc[BW + i] + pulled
        acc[p1] = acc[p1] + both[:, :BS]
        acc[p2] = acc[p2] + both[:, BS:]
    for i in range(nb):
        ss = split(ext[BW + i])
        ds = (ah[i], al[i])
        cols = slice(i * BS, (i + 1) * BS)
        img[:, cols] = acc[BW + i] + dot3(ss, ds, NT)
        imt[:, cols] = acc[BW + i] + dot3(ss, ds, NN)


def band_x_kernel(offs, s, a_hbm, o_hbm, img, imt, below, ah, al, oh, ol, ext, acc, a_ref, o_ref, sems):
    copies = (
        pltpu.make_async_copy(o_hbm, o_ref, sems.at[0]),
        pltpu.make_async_copy(a_hbm, a_ref, sems.at[1]),
    )
    for copy in copies:
        copy.start()
    for copy in copies:
        copy.wait()
    for i in range(ah.shape[0]):
        oh[i], ol[i] = split(lanes([o_ref[i, 0], o_ref[i, 1]]))
        ah[i], al[i] = split(a_ref[i])
    band_local(offs, s, ah, al, oh, ol, ext, acc, img, imt)
    for j in range(BW):
        below[:, j * BS : (j + 1) * BS] = acc[j]


def band_w_kernel(offs, s, ah, al, oh, ol, img, imt, ext, acc):
    band_local(offs, s, ah, al, oh, ol, ext, acc, img, imt)


def push_head(offs, s, oh, ol, push):
    for j in range(2 * BW):
        push[j] = jnp.zeros(push.shape[1:], F32)
    for i in range(BW):
        both = dot3(split(s[i]), (oh[i], ol[i]), NN)
        for k in range(2):
            at = BW + i - offs[k, i]
            push[at] = push[at] + both[:, k * BS : (k + 1) * BS]


def gram_kernel(count, nodes, offs, *refs):
    xs, ws = refs[:count], refs[count : 2 * count]
    (imgx, imtx, imgw, imtw, head, above, oh, ol, image, gram, left, right, hb) = refs[2 * count :]
    width = xs[0].shape[0]
    size = xs[0].shape[1]
    me = lax.axis_index("col")
    for j in range(BW):
        hb[j] = head[:, j * BS : (j + 1) * BS]
        hb[BW + j] = jnp.zeros((2 * width, BS), F32)
    for p, (img, imt) in enumerate(((imgx, imtx), (imgw, imtw))):
        rows = slice(p * width, (p + 1) * width)
        image[p] = img[...]
        image[p, :, size - TAIL :] = img[:, size - TAIL :] + above[rows]
        left[(2 + p) * width : (3 + p) * width] = imt[...]
        left[(2 + p) * width : (3 + p) * width, size - TAIL :] = imt[:, size - TAIL :] + above[rows]
        own = (xs, ws)[p][0]
        left[rows] = own[...]
        for k in range(count):
            at = jnp.bitwise_xor(me, k)
            right[pl.ds(pl.multiple_of((p * count + at) * width, width), width), :] = (xs, ws)[p][k][...]
    for i in range(BW):
        p1 = BW + i - offs[0, i]
        p2 = BW + i - offs[1, i]
        pulled = dot3(split(lanes([hb[p1], hb[p2]])), (oh[i], ol[i]), NT)
        cols = slice(i * BS, (i + 1) * BS)
        for p in range(2):
            part = pulled[p * width : (p + 1) * width]
            rows = slice((2 + p) * width, (3 + p) * width)
            image[p, :, cols] = image[p, :, cols] + part
            left[rows, cols] = left[rows, cols] + part
    gram[...] = dot3(split(left[...]), split(right[...]), NT) / nodes


def sum_kernel(*refs):
    parts, out = refs[:-1], refs[-1]
    whole = total(parts)
    width, half = out.shape[2], out.shape[4]
    for g in range(2):
        for p in range(2):
            at = (2 * g + p) * width
            for q in range(2):
                out[g, p, :, q, :] = whole[at : at + width, q * half : (q + 1) * half]


def call(kernel, outs, ins, smem=0, anys=0, last=0, scratch=(), flops=10**7):
    specs = [pl.BlockSpec(memory_space=pltpu.HBM)] * anys
    specs += [pl.BlockSpec(memory_space=pltpu.SMEM)] * smem
    specs += [pl.BlockSpec(memory_space=pltpu.VMEM)] * (len(ins) - smem - anys - last)
    specs += [pl.BlockSpec(memory_space=pltpu.HBM)] * last
    shapes = [jax.ShapeDtypeStruct(s, t) for s, t in outs]
    size = sum(a.size * a.dtype.itemsize for a in ins)
    return pl.pallas_call(
        kernel,
        out_shape=shapes,
        in_specs=specs,
        out_specs=[pl.BlockSpec(memory_space=pltpu.VMEM)] * len(shapes),
        scratch_shapes=scratch,
        cost_estimate=pl.CostEstimate(flops=flops, bytes_accessed=size, transcendentals=0),
        compiler_params=pltpu.CompilerParams(vmem_limit_bytes=32 * 2**20),
    )(*ins)


def gathered(value, axis):
    count = lax.axis_size(axis)
    parts = {0: value}
    step = count // 2
    while step:
        for k in list(parts):
            links = [(i, i ^ step) for i in range(count)]
            parts[k ^ step] = lax.ppermute(parts[k], axis, links)
        step //= 2
    return [parts[k] for k in range(count)]


def local_program(
    vectors, residual_block, diag_inverse, factor_blocks, band_diag, band_off, band_offsets
):
    width, size = vectors.shape
    nb = size // BS
    offsets = band_offsets.T
    slabs = lax.axis_size("slab")
    cols = lax.axis_size("col")
    pairs = slabs // 2
    rows = TAIL + width
    hrows = TAIL // 2 + width
    near = [(i, i ^ 1) for i in range(slabs)]
    cores = [(i, i ^ 1) for i in range(cols)]
    vec = ((width, TAIL), F32)
    flat = ((width, size), F32)
    matrix = [((2, TAIL, TAIL), BF)] * 2 + [((2, width, TAIL), F32)]

    mc, mch, c_own, zloc, fh, fl, bh, bl, dh, dl = call(
        prep_kernel,
        [((rows, TAIL), F32), ((hrows, TAIL), F32), vec, ((nb, width, BS), F32)]
        + [((nb + BW, rows, BS), BF)] * 2
        + [((nb, BS, 2 * BS), BF)] * 2
        + [((nb, BS, BS), BF)] * 2,
        [
            pltpu.with_memory_space_constraint(a, pltpu.HBM)
            for a in (offsets, diag_inverse, factor_blocks, residual_block)
        ],
        anys=4,
        scratch=[
            pltpu.SMEM(offsets.shape, jnp.int32),
            pltpu.VMEM(diag_inverse.shape, F32),
            pltpu.VMEM(factor_blocks.shape, F32),
            pltpu.VMEM(residual_block.shape, F32),
            pltpu.SemaphoreType.DMA((2, nb)),
            pltpu.SemaphoreType.DMA((2,)),
        ],
        flops=4 * 10**9,
    )
    c_got = lax.ppermute(c_own, "slab", [(0, 1)])
    m_near = lax.ppermute(mch, "slab", near)
    band_scratch = [pltpu.VMEM((nb + BW, width, BS), F32)] * 2
    imgx, imtx, belowx, ah, al, oh, ol = call(
        band_x_kernel,
        [flat, flat, vec] + [((nb, BS, BS), BF)] * 2 + [((nb, BS, 2 * BS), BF)] * 2,
        [offsets, vectors]
        + [pltpu.with_memory_space_constraint(a, pltpu.HBM) for a in (band_diag, band_off)],
        smem=1,
        last=2,
        scratch=band_scratch
        + [
            pltpu.VMEM(band_diag.shape, F32),
            pltpu.VMEM(band_off.shape, F32),
            pltpu.SemaphoreType.DMA((2,)),
        ],
        flops=10**9,
    )
    (t_out,) = call(early_kernel, [vec], [c_got, mc], flops=10**8)
    got_a = lax.ppermute(t_out, "slab", [(1, 3)])
    got_b = lax.ppermute(t_out, "slab", [(1, 2)])
    nd, ndh = call(
        energy_kernel, [((rows, TAIL), F32), ((hrows, TAIL), F32)], [fh, fl], flops=10**9
    )
    n_near = lax.ppermute(ndh, "slab", near)
    x_all = gathered(vectors, "col")
    up = [(i, i + 1) for i in range(slabs - 1)]
    down = [(i + 1, i) for i in range(slabs - 1)]
    m_other = lax.ppermute(m_near, "col", cores)
    n_other = lax.ppermute(n_near, "col", cores)

    mh, ml, c, t_out = call(
        first_kernel, matrix + [vec], [got_a, got_b, mc, m_near, m_other], flops=10**8
    )
    (composed,) = call(compose_kernel, [((TAIL // 2, TAIL), F32)], [mh, ml], flops=4 * 10**8)
    q_near = lax.ppermute(composed, "slab", [(2, 0), (3, 1)])
    q_other = lax.ppermute(q_near, "col", cores)
    ph, plow = call(join_kernel, [((TAIL, TAIL), BF)] * 2, [q_near, q_other], flops=10**6)
    nh, nl, d = call(assemble, matrix, [nd, n_near, n_other], flops=10**8)
    got = [got_a, got_b]
    for h in range(2, pairs):
        hop = [(2 * h - 2, 2 * h), (2 * h - 1, 2 * h + 1)]
        got.append(lax.ppermute(t_out, "slab", hop))
        if h < pairs - 1:
            kernel = functools.partial(forward_kernel, len(got))
            (t_out,) = call(kernel, [vec], got + [mh, ml, c], flops=10**8)
    e, u_out = call(
        functools.partial(turn_kernel, len(got)),
        [((2, width, TAIL), F32), vec],
        got + [mh, ml, c, nh, nl, d],
        flops=10**8,
    )
    (z,) = call(
        functools.partial(inner_kernel, len(got)),
        [((nb, width, BS), F32)],
        got + [mh, ml, c, fh, fl, zloc],
        flops=2 * 10**8,
    )
    got = []
    for h in range(pairs - 1, 1, -1):
        if h == 2:
            skip = lax.ppermute(u_out, "slab", [(4, 0), (5, 1)])
        hop = [(2 * h, 2 * h - 2), (2 * h + 1, 2 * h - 1)]
        if h == pairs - 1:
            e_out = u_out
            if h > 2:
                hop += [(2, 0), (3, 1)]
        got.append(lax.ppermute(u_out, "slab", hop))
        if h > 2:
            kernel = functools.partial(backward_kernel, len(got))
            (u_out,) = call(kernel, [vec], got + [mh, ml, e], flops=10**8)
    if pairs == 3:
        got.append(lax.ppermute(e_out, "slab", [(2, 0), (3, 1)]))
    n_got = len(got)

    def last_kernel(offs, *refs):
        solve_kernel(n_got, offs, *refs)

    half = nb // 2
    factors = [dh, dl, bh, bl]
    state = ((nb + BW, rows, BS), F32)
    q, kha, kla, va = call(
        upward_kernel,
        [state] + [((TAIL, (nb - half) * BS), BF)] * 2 + [((width, (nb - half) * BS), F32)],
        [offsets, z] + factors,
        smem=1,
        flops=2 * 10**9,
    )
    khb, klb, vb = call(
        upward_rest_kernel,
        [((TAIL, half * BS), BF)] * 2 + [((width, half * BS), F32)],
        [offsets, q] + factors,
        smem=1,
        scratch=[pltpu.VMEM(*state)],
        flops=2 * 10**9,
    )
    halo = ((2 * width, TAIL), F32)
    w, inner, tail, below = call(
        last_kernel,
        [flat, flat, halo, halo],
        [offsets]
        + got
        + [skip, ph, plow, mh, ml, e, va, kha, kla, vb, khb, klb, oh, ol, vectors, belowx],
        smem=1,
        scratch=[pltpu.VMEM((2 * BW, width, BS), F32)],
        flops=4 * 10**8,
    )
    w_all = gathered(inner, "col")
    head = lax.ppermute(tail, "slab", up)
    above = lax.ppermute(below, "slab", down)
    imgw, imtw = call(
        band_w_kernel,
        [flat, flat],
        [offsets, inner, ah, al, oh, ol],
        smem=1,
        scratch=band_scratch,
        flops=10**9,
    )
    image, gram = call(
        functools.partial(gram_kernel, cols, float(size * slabs)),
        [((2, width, size), F32), ((4 * width, 2 * cols * width), F32)],
        [offsets]
        + x_all
        + w_all
        + [imgx, imtx, imgw, imtw, head, above, oh, ol],
        smem=1,
        scratch=[
            pltpu.VMEM((4 * width, size), F32),
            pltpu.VMEM((2 * cols * width, size), F32),
            pltpu.VMEM((2 * BW, 2 * width, BS), F32),
        ],
        flops=10**9,
    )
    step = 1
    while step < slabs // 4:
        links = [(i, i ^ step) for i in range(slabs)]
        gram = gram + lax.ppermute(gram, "slab", links)
        step *= 2
    parts = [gram]
    for far in (step, 2 * step, 3 * step):
        parts.append(lax.ppermute(gram, "slab", [(i, i ^ far) for i in range(slabs)]))
    (gram,) = call(sum_kernel, [((2, 2, width, 2, cols * width), F32)], parts, flops=10**6)
    return (w, image, gram)


def solution(mesh):
    in_specs = (
        P("col", "slab"),
        P("col", "slab"),
        P("slab", None, None),
        P("slab", None, None, None),
        P("slab", None, None),
        P("slab", None, None, None),
        P("slab", None),
    )
    out_specs = (P("col", "slab"), P(None, "col", "slab"), P(None, None, "col", None, None))
    return jax.shard_map(
        local_program, mesh=mesh, in_specs=in_specs, out_specs=out_specs, check_vma=False
    )
```

```python
import functools

import jax
import jax.numpy as jnp
from jax import lax
from jax.experimental import pallas as pl
from jax.experimental.pallas import tpu as pltpu
from jax.sharding import PartitionSpec as P


BS = 128
BW = 3
TAIL = BW * BS
BF = jnp.bfloat16
F32 = jnp.float32
NN = (((1,), (0,)), ((), ()))
NT = (((1,), (1,)), ((), ()))


def split(a):
    hi = a.astype(BF)
    return hi, (a - hi.astype(F32)).astype(BF)


def mm(a, b, dims):
    return lax.dot_general(a, b, dims, preferred_element_type=F32)


def dot3(a, b, dims):
    (ah, al), (bh, bl) = a, b
    rows, depth = ah.shape
    if depth <= BS:
        axis = dims[0][1][0]
        twice = mm(jnp.concatenate([ah, al], 1), jnp.concatenate([bh, bh], axis), dims)
        return twice + mm(ah, bl, dims)
    both = mm(jnp.concatenate([ah, al], 0), bh, dims)
    return both[:rows] + (both[rows:] + mm(ah, bl, dims))


def lanes(parts):
    return jnp.concatenate(parts, 1)


def prep_kernel(offs_hbm, d_hbm, l_hbm, r_hbm, mc, mch, c_out, zloc, fh, fl, bh, bl, dh, dl, offs, d_ref, l_ref, r_ref, sems, other):
    nb = d_ref.shape[0]
    width = r_ref.shape[0]
    rows = TAIL + width
    copies = [(pltpu.make_async_copy(offs_hbm, offs, other.at[0]), pltpu.make_async_copy(r_hbm, r_ref, other.at[1]))]
    for i in range(nb):
        copies.append(
            (
                pltpu.make_async_copy(d_hbm.at[i], d_ref.at[i], sems.at[0, i]),
                pltpu.make_async_copy(l_hbm.at[i], l_ref.at[i], sems.at[1, i]),
            )
        )
    for pair in copies:
        for copy in pair:
            copy.start()
    half = lax.rem(lax.axis_index("col"), 2)
    row = lax.broadcasted_iota(jnp.int32, (rows, BS), 0)
    lane = lax.broadcasted_iota(jnp.int32, (rows, BS), 1)
    for j in range(BW):
        fh[j] = jnp.where(row == lane + j * BS, 1.0, 0.0).astype(BF)
        fl[j] = jnp.zeros((rows, BS), BF)
    for copy in copies[0]:
        copy.wait()

    def block(i):
        for copy in copies[1 + i]:
            copy.wait()
        ds = split(d_ref[i])
        bcat = split(dot3(ds, split(lanes([l_ref[i, 0], l_ref[i, 1]])), NN))
        bh[i], bl[i] = bcat
        dh[i], dl[i] = ds
        return bcat, dot3(split(r_ref[:, i * BS : (i + 1) * BS]), ds, NT)

    ahead = block(0)
    for i in range(nb):
        bcat, own = ahead
        if i + 1 < nb:
            ahead = block(i + 1)
        p1 = BW + i - offs[0, i]
        p2 = BW + i - offs[1, i]
        prev = (lanes([fh[p1], fh[p2]]), lanes([fl[p1], fl[p2]]))
        z = -dot3(prev, bcat, NT)
        z = jnp.concatenate([z[:TAIL], z[TAIL:] + own], 0)
        zloc[i] = z[TAIL:]
        zh, zl = split(z)
        fh[BW + i] = zh
        fl[BW + i] = zl
        if i >= nb - BW:
            k = i - (nb - BW)
            mc[:, k * BS : (k + 1) * BS] = z
    hr = TAIL // 2
    start = pl.multiple_of(half * hr, hr)
    mch[:hr] = mc[pl.ds(start, hr), :]
    mch[hr:] = mc[TAIL:, :]
    c_out[...] = mc[TAIL:, :]


def energy_kernel(fh, fl, nd, ndh):
    nb = fh.shape[0] - BW
    hr = TAIL // 2
    half = lax.rem(lax.axis_index("col"), 2)
    start = pl.multiple_of(half * hr, hr)
    ah = lanes([fh[BW + i] for i in range(nb)])
    al = lanes([fl[BW + i] for i in range(nb)])
    full = dot3((ah, al), (ah[:TAIL], al[:TAIL]), NT)
    nd[:TAIL] = full[:TAIL]
    nd[TAIL:] = -full[TAIL:]
    ndh[:hr] = nd[pl.ds(start, hr), :]
    ndh[hr:] = nd[TAIL:, :]


def early_kernel(c_got, mc, t_out):
    t_out[...] = mc[TAIL:] + dot3(split(c_got[...]), split(mc[:TAIL]), NN)


def assemble(own, near, other, high, low, vec):
    parity = lax.rem(lax.axis_index("slab"), 2)
    half = lax.rem(lax.axis_index("col"), 2)
    hr = TAIL // 2
    mine, theirs = parity, 1 - parity
    h, l = split(own[:TAIL])
    high[mine], low[mine] = h, l
    vec[mine] = own[TAIL:]
    vec[theirs] = near[hr:]
    for ref, which in ((near, half), (other, 1 - half)):
        h, l = split(ref[:hr])
        at = pl.ds(pl.multiple_of(which * hr, hr), hr)
        high[theirs, at, :] = h
        low[theirs, at, :] = l


def step_rows(x, high, low, slot, dims):
    return dot3(split(x), (high[slot], low[slot]), dims)


def first_kernel(got_a, got_b, own, near, other, high, low, vec, t_out):
    assemble(own, near, other, high, low, vec)
    mid = vec[0] + step_rows(got_a[...] + got_b[...], high, low, 0, NN)
    t_out[...] = vec[1] + step_rows(mid, high, low, 1, NN)


def total(refs):
    out = refs[0][...]
    for ref in refs[1:]:
        out = out + ref[...]
    return out


def forward_kernel(n, *refs):
    got, (high, low, vec, t_out) = refs[:n], refs[n:]
    mid = vec[0] + step_rows(total(got), high, low, 0, NN)
    t_out[...] = vec[1] + step_rows(mid, high, low, 1, NN)


def compose_kernel(high, low, half_out):
    hr = TAIL // 2
    start = pl.multiple_of(lax.rem(lax.axis_index("col"), 2) * hr, hr)
    mine = (high[0, pl.ds(start, hr), :], low[0, pl.ds(start, hr), :])
    half_out[...] = dot3(mine, (high[1], low[1]), NN)


def join_kernel(near, other, high, low):
    half = lax.rem(lax.axis_index("col"), 2)
    hr = TAIL // 2
    for ref, which in ((near, half), (other, 1 - half)):
        h, l = split(ref[...])
        at = pl.ds(pl.multiple_of(which * hr, hr), hr)
        high[at, :] = h
        low[at, :] = l


def turn_kernel(n, *refs):
    got, (mh, ml, c, nh, nl, d, e, u_out) = refs[:n], refs[n:]
    t_in = total(got)
    t_mid = c[0] + step_rows(t_in, mh, ml, 0, NN)
    e_odd = d[1] - step_rows(t_mid, nh, nl, 1, NN)
    e_even = d[0] - step_rows(t_in, nh, nl, 0, NN)
    e[0] = e_even
    e[1] = e_odd
    u_out[...] = step_rows(e_odd, mh, ml, 0, NT) + e_even


def inner_kernel(n, *refs):
    got, (mh, ml, c, fh, fl, zloc, z_out) = refs[:n], refs[n:]
    t_in = total(got)
    t_mid = c[0] + step_rows(t_in, mh, ml, 0, NN)
    odd = lax.rem(lax.axis_index("slab"), 2) == 1
    ts = split(jnp.where(odd, t_mid, t_in))
    for i in range(zloc.shape[0]):
        z_out[i] = zloc[i] + dot3(ts, (fh[BW + i, :TAIL], fl[BW + i, :TAIL]), NN)


def backward_kernel(n, *refs):
    got, (high, low, e, u_out) = refs[:n], refs[n:]
    mid = e[1] + step_rows(total(got), high, low, 1, NT)
    u_out[...] = step_rows(mid, high, low, 0, NT) + e[0]


def upward_steps(offs, dh, dl, bh, bl, q, kh, kl, v, blocks):
    first = blocks[0]
    for i in reversed(blocks):
        qs = split(q[BW + i])
        both = dot3(qs, (bh[i], bl[i]), NN)
        for k in range(2):
            at = BW + i - offs[k, i]
            q[at] = q[at] - both[:, k * BS : (k + 1) * BS]
        solved = dot3(qs, (dh[i], dl[i]), NN)
        cols = slice((i - first) * BS, (i - first + 1) * BS)
        v[:, cols] = solved[TAIL:]
        kh[:, cols], kl[:, cols] = split(solved[:TAIL])


def upward_kernel(offs, z, dh, dl, bh, bl, q, kh, kl, v):
    nb, width = z.shape[:2]
    row = lax.broadcasted_iota(jnp.int32, (TAIL, BS), 0)
    lane = lax.broadcasted_iota(jnp.int32, (TAIL, BS), 1)
    for i in range(nb + BW):
        q[i, :TAIL] = jnp.zeros((TAIL, BS), F32)
        if i >= nb:
            q[i, :TAIL] = jnp.where(row == lane + (i - nb) * BS, -1.0, 0.0)
        q[i, TAIL:] = z[i - BW] if i >= BW else jnp.zeros((width, BS), F32)
    upward_steps(offs, dh, dl, bh, bl, q, kh, kl, v, range(nb // 2, nb))


def upward_rest_kernel(offs, q_in, dh, dl, bh, bl, kh, kl, v, q):
    nb = dh.shape[0]
    for i in range(nb // 2 + BW):
        q[i] = q_in[i]
    upward_steps(offs, dh, dl, bh, bl, q, kh, kl, v, range(nb // 2))


def solve_kernel(n, offs, *refs):
    got, rest = refs[:n], refs[n:]
    (skip, ph, plow, high, low, e, va, kha, kla, vb, khb, klb, oh, ol, x, belowx) = rest[:16]
    (w, inner, inside, across, push) = rest[16:]
    _, size = x.shape
    odd = lax.rem(lax.axis_index("slab"), 2) == 1
    u_in = total(got) + dot3(split(skip[...]), (ph[...], plow[...]), NT)
    u_mid = e[1] + step_rows(u_in, high, low, 1, NT)
    u = jnp.where(odd, u_in, u_mid)
    us = split(u)
    solved = lanes(
        [
            vb[...] + dot3(us, (khb[...], klb[...]), NN),
            va[...] + dot3(us, (kha[...], kla[...]), NN),
        ]
    )
    w[...] = solved
    inner[...] = solved
    front = [solved[:, i * BS : (i + 1) * BS] for i in range(BW)]
    push_head(offs, front, oh, ol, push)
    tail = jnp.concatenate([x[:, size - TAIL :], solved[:, size - TAIL :]], 0)
    below = jnp.concatenate([belowx[...], lanes([push[j] for j in range(BW)])], 0)
    inside[...] = jnp.where(odd, below, tail)
    across[...] = jnp.where(odd, tail, below)


def band_local(offs, s, ah, al, oh, ol, ext, acc, img, imt):
    nb = ah.shape[0]
    width = s.shape[0]
    for j in range(BW):
        ext[j] = jnp.zeros((width, BS), F32)
    for j in range(nb + BW):
        acc[j] = jnp.zeros((width, BS), F32)
    for i in range(nb):
        ext[BW + i] = s[:, i * BS : (i + 1) * BS]
    for i in range(nb):
        ss = split(ext[BW + i])
        os = (oh[i], ol[i])
        p1 = BW + i - offs[0, i]
        p2 = BW + i - offs[1, i]
        pulled = dot3(split(lanes([ext[p1], ext[p2]])), os, NT)
        both = dot3(ss, os, NN)
        acc[BW + i] = acc[BW + i] + pulled
        acc[p1] = acc[p1] + both[:, :BS]
        acc[p2] = acc[p2] + both[:, BS:]
    for i in range(nb):
        ss = split(ext[BW + i])
        ds = (ah[i], al[i])
        cols = slice(i * BS, (i + 1) * BS)
        img[:, cols] = acc[BW + i] + dot3(ss, ds, NT)
        imt[:, cols] = acc[BW + i] + dot3(ss, ds, NN)


def band_x_kernel(offs, s, a_hbm, o_hbm, img, imt, below, ah, al, oh, ol, ext, acc, a_ref, o_ref, sems):
    copies = (
        pltpu.make_async_copy(o_hbm, o_ref, sems.at[0]),
        pltpu.make_async_copy(a_hbm, a_ref, sems.at[1]),
    )
    for copy in copies:
        copy.start()
    for copy in copies:
        copy.wait()
    for i in range(ah.shape[0]):
        oh[i], ol[i] = split(lanes([o_ref[i, 0], o_ref[i, 1]]))
        ah[i], al[i] = split(a_ref[i])
    band_local(offs, s, ah, al, oh, ol, ext, acc, img, imt)
    for j in range(BW):
        below[:, j * BS : (j + 1) * BS] = acc[j]


def band_w_kernel(offs, s, ah, al, oh, ol, img, imt, ext, acc):
    band_local(offs, s, ah, al, oh, ol, ext, acc, img, imt)


def push_head(offs, s, oh, ol, push):
    for j in range(2 * BW):
        push[j] = jnp.zeros(push.shape[1:], F32)
    for i in range(BW):
        both = dot3(split(s[i]), (oh[i], ol[i]), NN)
        for k in range(2):
            at = BW + i - offs[k, i]
            push[at] = push[at] + both[:, k * BS : (k + 1) * BS]


def gram_kernel(count, nodes, offs, *refs):
    xs, ws = refs[:count], refs[count : 2 * count]
    (imgx, imtx, imgw, imtw, inside, across, oh, ol, image, gram, left, right, hb) = refs[2 * count :]
    width = xs[0].shape[0]
    size = xs[0].shape[1]
    me = lax.axis_index("col")
    odd = lax.rem(lax.axis_index("slab"), 2) == 1
    head = jnp.where(odd, inside[...], across[...])
    above = jnp.where(odd, across[...], inside[...])
    for j in range(BW):
        hb[j] = head[:, j * BS : (j + 1) * BS]
        hb[BW + j] = jnp.zeros((2 * width, BS), F32)
    for p, (img, imt) in enumerate(((imgx, imtx), (imgw, imtw))):
        rows = slice(p * width, (p + 1) * width)
        image[p] = img[...]
        image[p, :, size - TAIL :] = img[:, size - TAIL :] + above[rows]
        left[(2 + p) * width : (3 + p) * width] = imt[...]
        left[(2 + p) * width : (3 + p) * width, size - TAIL :] = imt[:, size - TAIL :] + above[rows]
        own = (xs, ws)[p][0]
        left[rows] = own[...]
        for k in range(count):
            at = jnp.bitwise_xor(me, k)
            right[pl.ds(pl.multiple_of((p * count + at) * width, width), width), :] = (xs, ws)[p][k][...]
    for i in range(BW):
        p1 = BW + i - offs[0, i]
        p2 = BW + i - offs[1, i]
        pulled = dot3(split(lanes([hb[p1], hb[p2]])), (oh[i], ol[i]), NT)
        cols = slice(i * BS, (i + 1) * BS)
        for p in range(2):
            part = pulled[p * width : (p + 1) * width]
            rows = slice((2 + p) * width, (3 + p) * width)
            image[p, :, cols] = image[p, :, cols] + part
            left[rows, cols] = left[rows, cols] + part
    gram[...] = dot3(split(left[...]), split(right[...]), NT) / nodes


def sum_kernel(*refs):
    parts, out = refs[:-1], refs[-1]
    whole = total(parts)
    width, half = out.shape[2], out.shape[4]
    for g in range(2):
        for p in range(2):
            at = (2 * g + p) * width
            for q in range(2):
                out[g, p, :, q, :] = whole[at : at + width, q * half : (q + 1) * half]


def call(kernel, outs, ins, smem=0, anys=0, last=0, scratch=(), flops=10**7):
    specs = [pl.BlockSpec(memory_space=pltpu.HBM)] * anys
    specs += [pl.BlockSpec(memory_space=pltpu.SMEM)] * smem
    specs += [pl.BlockSpec(memory_space=pltpu.VMEM)] * (len(ins) - smem - anys - last)
    specs += [pl.BlockSpec(memory_space=pltpu.HBM)] * last
    shapes = [jax.ShapeDtypeStruct(s, t) for s, t in outs]
    size = sum(a.size * a.dtype.itemsize for a in ins)
    return pl.pallas_call(
        kernel,
        out_shape=shapes,
        in_specs=specs,
        out_specs=[pl.BlockSpec(memory_space=pltpu.VMEM)] * len(shapes),
        scratch_shapes=scratch,
        cost_estimate=pl.CostEstimate(flops=flops, bytes_accessed=size, transcendentals=0),
        compiler_params=pltpu.CompilerParams(vmem_limit_bytes=32 * 2**20),
    )(*ins)


def gathered(value, axis):
    count = lax.axis_size(axis)
    parts = {0: value}
    step = count // 2
    while step:
        for k in list(parts):
            links = [(i, i ^ step) for i in range(count)]
            parts[k ^ step] = lax.ppermute(parts[k], axis, links)
        step //= 2
    return [parts[k] for k in range(count)]


def local_program(
    vectors, residual_block, diag_inverse, factor_blocks, band_diag, band_off, band_offsets
):
    width, size = vectors.shape
    nb = size // BS
    offsets = band_offsets.T
    slabs = lax.axis_size("slab")
    cols = lax.axis_size("col")
    pairs = slabs // 2
    rows = TAIL + width
    hrows = TAIL // 2 + width
    near = [(i, i ^ 1) for i in range(slabs)]
    cores = [(i, i ^ 1) for i in range(cols)]
    vec = ((width, TAIL), F32)
    flat = ((width, size), F32)
    matrix = [((2, TAIL, TAIL), BF)] * 2 + [((2, width, TAIL), F32)]

    mc, mch, c_own, zloc, fh, fl, bh, bl, dh, dl = call(
        prep_kernel,
        [((rows, TAIL), F32), ((hrows, TAIL), F32), vec, ((nb, width, BS), F32)]
        + [((nb + BW, rows, BS), BF)] * 2
        + [((nb, BS, 2 * BS), BF)] * 2
        + [((nb, BS, BS), BF)] * 2,
        [
            pltpu.with_memory_space_constraint(a, pltpu.HBM)
            for a in (offsets, diag_inverse, factor_blocks, residual_block)
        ],
        anys=4,
        scratch=[
            pltpu.SMEM(offsets.shape, jnp.int32),
            pltpu.VMEM(diag_inverse.shape, F32),
            pltpu.VMEM(factor_blocks.shape, F32),
            pltpu.VMEM(residual_block.shape, F32),
            pltpu.SemaphoreType.DMA((2, nb)),
            pltpu.SemaphoreType.DMA((2,)),
        ],
        flops=4 * 10**9,
    )
    c_got = lax.ppermute(c_own, "slab", [(0, 1)])
    m_near = lax.ppermute(mch, "slab", near)
    band_scratch = [pltpu.VMEM((nb + BW, width, BS), F32)] * 2
    imgx, imtx, belowx, ah, al, oh, ol = call(
        band_x_kernel,
        [flat, flat, vec] + [((nb, BS, BS), BF)] * 2 + [((nb, BS, 2 * BS), BF)] * 2,
        [offsets, vectors]
        + [pltpu.with_memory_space_constraint(a, pltpu.HBM) for a in (band_diag, band_off)],
        smem=1,
        last=2,
        scratch=band_scratch
        + [
            pltpu.VMEM(band_diag.shape, F32),
            pltpu.VMEM(band_off.shape, F32),
            pltpu.SemaphoreType.DMA((2,)),
        ],
        flops=10**9,
    )
    (t_out,) = call(early_kernel, [vec], [c_got, mc], flops=10**8)
    got_a = lax.ppermute(t_out, "slab", [(1, 3)])
    got_b = lax.ppermute(t_out, "slab", [(1, 2)])
    nd, ndh = call(
        energy_kernel, [((rows, TAIL), F32), ((hrows, TAIL), F32)], [fh, fl], flops=10**9
    )
    n_near = lax.ppermute(ndh, "slab", near)
    x_all = gathered(vectors, "col")
    m_other = lax.ppermute(m_near, "col", cores)
    n_other = lax.ppermute(n_near, "col", cores)

    mh, ml, c, t_out = call(
        first_kernel, matrix + [vec], [got_a, got_b, mc, m_near, m_other], flops=10**8
    )
    (composed,) = call(compose_kernel, [((TAIL // 2, TAIL), F32)], [mh, ml], flops=4 * 10**8)
    q_near = lax.ppermute(composed, "slab", [(2, 0), (3, 1)])
    q_other = lax.ppermute(q_near, "col", cores)
    ph, plow = call(join_kernel, [((TAIL, TAIL), BF)] * 2, [q_near, q_other], flops=10**6)
    nh, nl, d = call(assemble, matrix, [nd, n_near, n_other], flops=10**8)
    got = [got_a, got_b]
    for h in range(2, pairs):
        hop = [(2 * h - 2, 2 * h), (2 * h - 1, 2 * h + 1)]
        got.append(lax.ppermute(t_out, "slab", hop))
        if h < pairs - 1:
            kernel = functools.partial(forward_kernel, len(got))
            (t_out,) = call(kernel, [vec], got + [mh, ml, c], flops=10**8)
    e, u_out = call(
        functools.partial(turn_kernel, len(got)),
        [((2, width, TAIL), F32), vec],
        got + [mh, ml, c, nh, nl, d],
        flops=10**8,
    )
    (z,) = call(
        functools.partial(inner_kernel, len(got)),
        [((nb, width, BS), F32)],
        got + [mh, ml, c, fh, fl, zloc],
        flops=2 * 10**8,
    )
    got = []
    for h in range(pairs - 1, 1, -1):
        if h == 2:
            skip = lax.ppermute(u_out, "slab", [(4, 0), (5, 1)])
        hop = [(2 * h, 2 * h - 2), (2 * h + 1, 2 * h - 1)]
        if h == pairs - 1:
            e_out = u_out
            if h > 2:
                hop += [(2, 0), (3, 1)]
        got.append(lax.ppermute(u_out, "slab", hop))
        if h > 2:
            kernel = functools.partial(backward_kernel, len(got))
            (u_out,) = call(kernel, [vec], got + [mh, ml, e], flops=10**8)
    if pairs == 3:
        got.append(lax.ppermute(e_out, "slab", [(2, 0), (3, 1)]))
    n_got = len(got)

    def last_kernel(offs, *refs):
        solve_kernel(n_got, offs, *refs)

    half = nb // 2
    factors = [dh, dl, bh, bl]
    state = ((nb + BW, rows, BS), F32)
    q, kha, kla, va = call(
        upward_kernel,
        [state] + [((TAIL, (nb - half) * BS), BF)] * 2 + [((width, (nb - half) * BS), F32)],
        [offsets, z] + factors,
        smem=1,
        flops=2 * 10**9,
    )
    khb, klb, vb = call(
        upward_rest_kernel,
        [((TAIL, half * BS), BF)] * 2 + [((width, half * BS), F32)],
        [offsets, q] + factors,
        smem=1,
        scratch=[pltpu.VMEM(*state)],
        flops=2 * 10**9,
    )
    halo = ((2 * width, TAIL), F32)
    w, inner, inside, across = call(
        last_kernel,
        [flat, flat, halo, halo],
        [offsets]
        + got
        + [skip, ph, plow, mh, ml, e, va, kha, kla, vb, khb, klb, oh, ol, vectors, belowx],
        smem=1,
        scratch=[pltpu.VMEM((2 * BW, width, BS), F32)],
        flops=4 * 10**8,
    )
    w_all = gathered(inner, "col")
    inside = lax.ppermute(inside, "slab", near)
    between = [(i, i + 1) for i in range(1, slabs - 1, 2)]
    across = lax.ppermute(across, "slab", between + [(j, i) for i, j in between])
    imgw, imtw = call(
        band_w_kernel,
        [flat, flat],
        [offsets, inner, ah, al, oh, ol],
        smem=1,
        scratch=band_scratch,
        flops=10**9,
    )
    image, gram = call(
        functools.partial(gram_kernel, cols, float(size * slabs)),
        [((2, width, size), F32), ((4 * width, 2 * cols * width), F32)],
        [offsets]
        + x_all
        + w_all
        + [imgx, imtx, imgw, imtw, inside, across, oh, ol],
        smem=1,
        scratch=[
            pltpu.VMEM((4 * width, size), F32),
            pltpu.VMEM((2 * cols * width, size), F32),
            pltpu.VMEM((2 * BW, 2 * width, BS), F32),
        ],
        flops=10**9,
    )
    step = 1
    while step < slabs // 4:
        links = [(i, i ^ step) for i in range(slabs)]
        gram = gram + lax.ppermute(gram, "slab", links)
        step *= 2
    parts = [gram]
    for far in (step, 2 * step, 3 * step):
        parts.append(lax.ppermute(gram, "slab", [(i, i ^ far) for i in range(slabs)]))
    (gram,) = call(sum_kernel, [((2, 2, width, 2, cols * width), F32)], parts, flops=10**6)
    return (w, image, gram)


def solution(mesh):
    in_specs = (
        P("col", "slab"),
        P("col", "slab"),
        P("slab", None, None),
        P("slab", None, None, None),
        P("slab", None, None),
        P("slab", None, None, None),
        P("slab", None),
    )
    out_specs = (P("col", "slab"), P(None, "col", "slab"), P(None, None, "col", None, None))
    return jax.shard_map(
        local_program, mesh=mesh, in_specs=in_specs, out_specs=out_specs, check_vma=False
    )
```
